32 devices in a mesh: tile: 8 (over y, x, core), gene: 4 (over z).
Axes of the slice: x: 2, y: 2, z: 4, core: 2. Of those that a mesh axis runs over, the one named last changes fastest.
Arguments:
- features: bfloat16 [64, 256, 1536], P('tile'), may hold values from -6 to 6
- counts: int32 [64, 256, 4096], P('tile', None, 'gene'), may hold values from 0 to 12
- selection: int32 [32, 4], P('gene'), may hold values from 0 to 11, as said below
- weights: bfloat16 [4608, 4096], P('tile', 'gene'), may hold values from -0.09375 to 0.09375
Outputs:
- grad_weights: float32 [4608, 4096], P('tile', 'gene')
The draws below stay inside these ranges and needn't reach their ends.
Inputs may be any that keep to these rules, and one draw needn't show every extreme that they name: `selection`: each row names 4 different feature blocks.
All inputs are finite; a program needn't handle non-finite values.
Results may differ from the reference program's by a relative error of at most 0.0038.
Values may be sent and summed in bfloat16 or wider, within the bound.
No kernel may reach another device: no remote copies, remote signals or barrier semaphores. Data moves between devices by JAX's collectives and lax.ppermute only.
A program may use at most 576 MiB of HBM per device.

```python
import math
import jax
import jax.numpy as jnp
from jax import lax

FEATURES = 1536
GENES = 4096
READ_BLOCKS = 4
GRID_COLS = 256
GRID_ROWS = 64
GENE_BLOCKS = 32
WINDOW_WIDTH = 4608


def draw_counts(key, part):
    gene_index = jnp.arange(GENES, dtype=jnp.int32)
    ceiling = 2 + 12 * gene_index // GENES
    return jax.random.randint(key, (GRID_ROWS, GRID_COLS, GENES), 0, ceiling, dtype=jnp.int32)


def draw_selection(key, part):
    key_list = jax.random.split(key, GENE_BLOCKS)

    def one_row(row_key):
        return jax.random.permutation(row_key, FEATURES // 128)[:READ_BLOCKS]
    return jax.vmap(one_row)(key_list).astype(jnp.int32)


def shard_levels(key, dims, cuts, smallest, high):
    gain, own = 1.0, jax.random.fold_in(key, 6)
    for position, parts in cuts:
        draws = jnp.exp(jax.random.uniform(jax.random.fold_in(own, position), (parts,), jnp.float32, smallest / len(cuts), high / len(cuts)))
        gain = gain * jnp.repeat(draws, dims[position] // parts).reshape([-1 if axis == position else 1 for axis in range(len(dims))])
    return gain


def bell_draw(stream_key, shape, deviation, most, cuts=(), kind=jnp.bfloat16):
    array = jax.random.normal(stream_key, shape, jnp.float32) * deviation
    if len(cuts) > 0:
        array = shard_levels(stream_key, shape, cuts, -0.22, 0.18) * array
    return jnp.clip(array, min=-most, max=most).astype(kind)


def setup_inputs(seed: int = 0) -> dict:
    streams_of = jax.random.split(jax.random.key(seed), 5)
    features = bell_draw(streams_of[0], (GRID_ROWS, GRID_COLS, FEATURES), 1.0, 6.0, ((0, 8),))
    counts = draw_counts(jax.random.fold_in(streams_of[4], 71), 0)
    selection = draw_selection(jax.random.fold_in(streams_of[4], 71), 0)
    weights = bell_draw(streams_of[3], (WINDOW_WIDTH, GENES), WINDOW_WIDTH ** -0.5, 0.09375, ((0, 8), (1, 4)))
    return dict(features=features, counts=counts, selection=selection, weights=weights)


def take_window(padded, chosen, row_count, col_count):
    col_blocks = [lax.dynamic_slice_in_dim(padded, (chosen[feat_slot] * 128).astype(jnp.int32), 128, 2) for feat_slot in range(chosen.shape[0])]
    pieces = []
    for row_step in (-1, 0, 1):
        for col_step in (-1, 0, 1):
            for col_block in col_blocks:
                pieces.append(col_block[1 + row_step:1 + row_step + row_count, 1 + col_step:1 + col_step + col_count, :])
    return jnp.concatenate(pieces, axis=2).reshape(row_count * col_count, -1)

def reference(features, counts, selection, weights):
    grid_rows, grid_cols, feat_width = features.shape
    gene_count = counts.shape[2]
    blocks = gene_count // 128
    bin_count = grid_rows * grid_cols
    norm_scale = 1.0 / math.sqrt(bin_count)
    padded = jnp.pad(features, ((1, 1), (1, 1), (0, 0)))
    library = lax.optimization_barrier(jnp.sum(counts.astype(jnp.float32), axis=2)) + 1.0
    size_factor = (library / gene_count).reshape(bin_count, 1)
    weight_blocks = weights.reshape(-1, blocks, 128).transpose(1, 0, 2)
    count_blocks = counts.reshape(bin_count, blocks, 128).transpose(1, 0, 2)

    def one_block(block_items):
        chosen, weight_block, count_block = block_items
        window = take_window(padded, chosen, grid_rows, grid_cols)
        logits = jnp.dot(window, weight_block, preferred_element_type=jnp.float32)
        expected = size_factor * jnp.exp(logits)
        excess = (expected - count_block.astype(jnp.float32)).astype(jnp.bfloat16)
        return lax.dot_general(window, excess, (((0,), (0,)), ((), ())), preferred_element_type=jnp.float32) * norm_scale
    gradients = lax.map(one_block, (selection, weight_blocks, count_blocks))
    return gradients.transpose(1, 0, 2).reshape(-1, gene_count)
```

```python
import functools
import math

import jax
import jax.numpy as jnp
from jax import lax
from jax.experimental import pallas as pl
from jax.experimental.pallas import tpu as pltpu
from jax.sharding import PartitionSpec as P

LANES = 128
STEPS = 3
CHUNKS = (1, 1, 2)

NT = (((1,), (1,)), ((), ()))
ANY = pl.BlockSpec(memory_space=pl.ANY)


def swap_cores(x, count):
    return lax.ppermute(x, "tile", [(t, t ^ 1) for t in range(count)])


def swap_chips(x, bit, count):
    return lax.ppermute(x, "tile", [(t, t ^ (2 << bit)) for t in range(count)])


def counts_kernel(counts_ref, turned_ref, library_ref):
    block = counts_ref[0].astype(jnp.float32).T
    turned_ref[...] = block.astype(jnp.bfloat16)
    library_ref[...] = jnp.sum(block, axis=0, keepdims=True)


def turn_counts(counts):
    row_count, col_count, genes = counts.shape
    bins = row_count * col_count
    return pl.pallas_call(
        counts_kernel,
        grid=(row_count,),
        in_specs=[pl.BlockSpec((1, col_count, genes), lambda r: (r, 0, 0))],
        out_specs=[
            pl.BlockSpec((genes, col_count), lambda r: (0, r)),
            pl.BlockSpec((1, col_count), lambda r: (0, r)),
        ],
        out_shape=[
            jax.ShapeDtypeStruct((genes, bins), jnp.bfloat16),
            jax.ShapeDtypeStruct((1, bins), jnp.float32),
        ],
        name="turn_counts",
        cost_estimate=pl.CostEstimate(flops=0, bytes_accessed=counts.size * 6, transcendentals=0),
    )(counts)


def grad_kernel(
    dims, scalars, selection, f_own, f_other, h_came, h_swapped, c_own, c_other, l_own, l_other, *rest
):
    own_rows, cols, pieces, piece_blocks, halves, gene_total = dims
    parts = pieces * halves
    w_parts, g_parts = rest[:parts], rest[parts : 2 * parts]
    fs, wv, cs, ls, wl, et, acc, gb, in_sem, out_sem = rest[2 * parts :]
    step, steps = pl.program_id(0), pl.num_programs(0)
    core = scalars[0]
    own_bins = own_rows * cols
    rows = 2 * own_rows
    reads = selection.shape[1]
    half = LANES // halves

    def loads(j, slot):
        copies = []
        for k in range(reads):
            lane = pl.multiple_of(selection[j, k] * LANES, LANES)
            target = pl.ds(k * LANES, LANES)
            for source, at, size in (
                (f_own, cols + core * own_bins, own_bins),
                (f_other, cols + (1 - core) * own_bins, own_bins),
                (h_came, core * (rows + 1) * cols, cols),
                (h_swapped, (1 - core) * (rows + 1) * cols, cols),
            ):
                at = pl.multiple_of(at, cols)
                copies.append((source.at[:, pl.ds(lane, LANES)], fs.at[slot, pl.ds(at, size), target]))
        for p in range(pieces):
            first = scalars[1 + p] * piece_blocks
            for h in range(halves):
                copies.append(
                    (
                        w_parts[p * halves + h].at[j],
                        wv.at[slot, pl.ds(first, piece_blocks), pl.ds(h * half, half)],
                    )
                )
        genes = pl.ds(pl.multiple_of(j * LANES, LANES), LANES)
        for source, at in ((c_own, core * own_bins), (c_other, (1 - core) * own_bins)):
            at = pl.multiple_of(at, own_bins)
            copies.append((source.at[genes], cs.at[slot, :, pl.ds(at, own_bins)]))
        return [
            pltpu.make_async_copy(source, target, in_sem.at[slot, i])
            for i, (source, target) in enumerate(copies)
        ]

    def stores(j):
        copies = []
        for p in range(pieces):
            first = scalars[1 + p] * piece_blocks
            for h in range(halves):
                copies.append(
                    (gb.at[pl.ds(first, piece_blocks), pl.ds(h * half, half)], g_parts[p * halves + h].at[j])
                )
        return [
            pltpu.make_async_copy(source, target, out_sem.at[i])
            for i, (source, target) in enumerate(copies)
        ]

    slot = lax.rem(step, 2)

    @pl.when(step == 0)
    def _():
        for copy in loads(0, 0):
            copy.start()
        ls[:, pl.ds(pl.multiple_of(core * own_bins, own_bins), own_bins)] = l_own[...]
        ls[:, pl.ds(pl.multiple_of((1 - core) * own_bins, own_bins), own_bins)] = l_other[...]
        ls[...] = (ls[...] + 1.0) / gene_total

    @pl.when(step + 1 < steps)
    def _():
        for copy in loads(step + 1, 1 - slot):
            copy.start()

    for copy in loads(step, slot):
        copy.wait()

    for d in range(STEPS):
        for e in range(STEPS):
            for k in range(reads):
                wl[d, e * LANES : (e + 1) * LANES, k * LANES : (k + 1) * LANES] = wv[
                    slot, (STEPS * d + e) * reads + k
                ]

    lane = lax.broadcasted_iota(jnp.int32, (LANES, cols), 1)

    def from_left(x):
        return jnp.where(lane > 0, pltpu.roll(x, 1, 1), 0.0)

    def from_right(x):
        return jnp.where(lane < cols - 1, pltpu.roll(x, cols - 1, 1), 0.0)

    def products(r):
        total = None
        for d in range(STEPS):
            one = lax.dot_general(
                wl[d], fs[slot, pl.ds((r + d) * cols, cols), :], NT, preferred_element_type=jnp.float32
            )
            total = one if total is None else total + one
        return total

    def finish(r, sums):
        here = slice(r * cols, (r + 1) * cols)
        logits = (
            from_left(sums[:LANES]) + sums[LANES : 2 * LANES] + from_right(sums[2 * LANES :])
        )
        excess = ls[:, here] * jnp.exp(logits) - cs[slot, :, here].astype(jnp.float32)
        et[:LANES, here] = from_right(excess).astype(jnp.bfloat16)
        et[LANES : 2 * LANES, here] = excess.astype(jnp.bfloat16)
        et[2 * LANES :, here] = from_left(excess).astype(jnp.bfloat16)

    acc[0] = products(0)
    for r in range(1, rows):
        acc[r % 2] = products(r)
        finish(r - 1, acc[(r - 1) % 2])
    finish(rows - 1, acc[(rows - 1) % 2])

    @pl.when(step > 0)
    def _():
        for copy in stores(step - 1):
            copy.wait()

    for d in range(STEPS):
        grad = jnp.dot(
            et[...], fs[slot, d * cols : (d + rows) * cols, :], preferred_element_type=jnp.float32
        )
        for e in range(STEPS):
            for k in range(reads):
                gb[(STEPS * d + e) * reads + k] = grad[
                    e * LANES : (e + 1) * LANES, k * LANES : (k + 1) * LANES
                ].astype(jnp.bfloat16)

    for copy in stores(step):
        copy.start()

    @pl.when(step + 1 == steps)
    def _():
        for copy in stores(step):
            copy.wait()


def chunk_gradient(
    scalars, selection, features, halos, counts, libraries, w_parts, pieces, halves, own_rows, cols, gene_total
):
    blocks, reads = selection.shape
    rows = 2 * own_rows
    taps = STEPS * STEPS * reads
    piece_blocks = taps // pieces
    dims = (own_rows, cols, pieces, piece_blocks, halves, gene_total)
    n_in = 4 * reads + pieces * halves + 2
    bins = rows * cols
    vmem = pl.BlockSpec(memory_space=pltpu.VMEM)
    flops = 4 * blocks * taps * LANES * LANES * bins
    return pl.pallas_call(
        functools.partial(grad_kernel, dims),
        grid_spec=pltpu.PrefetchScalarGridSpec(
            num_scalar_prefetch=2,
            grid=(blocks,),
            in_specs=[ANY] * 6 + [vmem] * 2 + [ANY] * (pieces * halves),
            out_specs=[ANY] * (pieces * halves),
            scratch_shapes=[
                pltpu.VMEM((2, bins + 2 * cols, reads * LANES), jnp.bfloat16),
                pltpu.VMEM((2, taps, LANES, LANES), jnp.bfloat16),
                pltpu.VMEM((2, LANES, bins), jnp.bfloat16),
                pltpu.VMEM((1, bins), jnp.float32),
                pltpu.VMEM((STEPS, STEPS * LANES, reads * LANES), jnp.bfloat16),
                pltpu.VMEM((STEPS * LANES, bins), jnp.bfloat16),
                pltpu.VMEM((2, STEPS * LANES, cols), jnp.float32),
                pltpu.VMEM((taps, LANES, LANES), jnp.bfloat16),
                pltpu.SemaphoreType.DMA((2, n_in)),
                pltpu.SemaphoreType.DMA((pieces * halves,)),
            ],
        ),
        out_shape=[jax.ShapeDtypeStruct(w.shape, jnp.bfloat16) for w in w_parts],
        compiler_params=pltpu.CompilerParams(vmem_limit_bytes=40 << 20),
        name="chunk_gradient",
        cost_estimate=pl.CostEstimate(
            flops=flops, bytes_accessed=blocks * 8 * 2**20, transcendentals=blocks * LANES * bins
        ),
    )(scalars, selection, *features, *halos, *counts, *libraries, *w_parts)


def tapped(part, genes):
    return part.reshape(-1, LANES, genes // LANES, LANES).transpose(2, 0, 3, 1)


def untapped(part):
    blocks, row_blocks = part.shape[:2]
    return part.transpose(1, 3, 0, 2).reshape(row_blocks * LANES, blocks * LANES)


def gather_chips(part, count):
    a, b = part[:, :, : LANES // 2], part[:, :, LANES // 2 :]
    a1, b2 = swap_chips(a, 0, count), swap_chips(b, 1, count)
    a2, b1 = swap_chips(a, 1, count), swap_chips(b, 0, count)
    a3, b3 = swap_chips(a1, 1, count), swap_chips(b2, 0, count)
    return [a, b, a1, b1, a2, b2, a3, b3]


def add(x, y):
    return x.astype(jnp.float32) + y.astype(jnp.float32)


def reduce_chips(parts, count):
    a, b, a1, b1, a2, b2, a3, b3 = parts
    to_a1, to_b2 = swap_chips(a3, 1, count), swap_chips(b3, 0, count)
    to_a, to_b = swap_chips(a2, 1, count), swap_chips(b1, 0, count)
    a1 = add(a1, to_a1).astype(jnp.bfloat16)
    b2 = add(b2, to_b2).astype(jnp.bfloat16)
    last_a, last_b = swap_chips(a1, 0, count), swap_chips(b2, 1, count)
    a = add(a, to_a) + last_a.astype(jnp.float32)
    b = add(b, to_b) + last_b.astype(jnp.float32)
    return jnp.concatenate([a, b], axis=2)


def per_device(features, counts, selection, weights):
    row_count, col_count, width = features.shape
    local_genes = counts.shape[2]
    tiles, gene_parts = lax.axis_size("tile"), lax.axis_size("gene")
    gene_total = local_genes * gene_parts
    norm_scale = 1.0 / math.sqrt(row_count * tiles * col_count)
    bins = row_count * col_count
    me = lax.axis_index("tile")
    core, chip = me % 2, me // 2
    core_genes = local_genes // 2
    core_blocks = core_genes // LANES
    share = weights.shape[0]
    chips = tiles // 2
    planned = chips == 4 and (2 * share) % LANES == 0 and sum(CHUNKS) == core_blocks
    chunks = CHUNKS if planned else (core_blocks,)

    def split_cols(x, size, base=0):
        mine = lax.dynamic_slice_in_dim(x, core * core_genes + base, size, 1)
        other = lax.dynamic_slice_in_dim(x, (1 - core) * core_genes + base, size, 1)
        return mine, other

    gathered = []
    base = 0
    for size in chunks:
        genes = size * LANES
        if planned:
            mine, other = split_cols(weights, genes, base * LANES)
            came = swap_cores(other, tiles)
            low = jnp.where(core == 0, mine, came)
            high = jnp.where(core == 0, came, mine)
            rows = jnp.concatenate([low, high], axis=0)
            gathered.append(gather_chips(tapped(rows, genes), tiles))
        else:
            full = lax.all_gather(weights, "tile", axis=0, tiled=True)
            gathered.append([tapped(split_cols(full, genes)[0], genes)])
        base += size

    flat = features.reshape(bins, width)
    other_rows = swap_cores(flat, tiles)
    edge = jnp.where(core == 0, features[0], features[row_count - 1])
    outward = [(t, t + 1) for t in range(1, tiles - 1, 2)] + [(t, t - 1) for t in range(2, tiles, 2)]
    halo = lax.ppermute(edge, "tile", outward)
    other_halo = swap_cores(halo, tiles)

    turned, library = turn_counts(counts)
    own_counts = lax.dynamic_slice_in_dim(turned, core * core_genes, core_genes, 0)
    other_counts = swap_cores(
        lax.dynamic_slice_in_dim(turned, (1 - core) * core_genes, core_genes, 0), tiles
    )
    if gene_parts & (gene_parts - 1) == 0:
        bit = 1
        while bit < gene_parts:
            library += lax.ppermute(library, "gene", [(g, g ^ bit) for g in range(gene_parts)])
            bit *= 2
    else:
        library = lax.psum(library, "gene")
    other_library = swap_cores(library, tiles)

    own_selection = lax.dynamic_slice_in_dim(selection, core * core_blocks, core_blocks, 0)
    if planned:
        pieces, halves = chips, 2
        places = [chip ^ p for p in range(chips)]
    else:
        pieces, halves = 1, 1
        places = [jnp.zeros_like(chip)]
    scalars = jnp.stack([core] + places).astype(jnp.int32)

    sums = []
    base = 0
    for size, w_parts in zip(chunks, gathered):
        genes = slice(base * LANES, (base + size) * LANES)
        parts = chunk_gradient(
            scalars,
            own_selection[base : base + size],
            (flat, other_rows),
            (halo, other_halo),
            (own_counts[genes], other_counts[genes]),
            (library, other_library),
            w_parts,
            pieces,
            halves,
            row_count,
            col_count,
            gene_total,
        )
        base += size
        if planned:
            total = untapped(reduce_chips(parts, tiles)) * norm_scale
            mine = lax.dynamic_slice_in_dim(total, core * share, share, 0)
            other = lax.dynamic_slice_in_dim(total, (1 - core) * share, share, 0)
            came = swap_cores(other, tiles)
            sums.append((jnp.where(core == 0, mine, came), jnp.where(core == 0, came, mine)))
        else:
            part = untapped(parts[0]).astype(jnp.float32)
            nothing = jnp.zeros_like(part)
            low, high = jnp.where(core == 0, part, nothing), jnp.where(core == 0, nothing, part)
            total = lax.psum_scatter(
                jnp.concatenate([low, high], axis=1), "tile", scatter_dimension=0, tiled=True
            )
            return total * norm_scale
    return jnp.concatenate([low for low, _ in sums] + [high for _, high in sums], axis=1)


def solution(mesh):
    in_specs = (P("tile", None, None), P("tile", None, "gene"), P("gene", None), P("tile", "gene"))
    out_specs = P("tile", "gene")
    return jax.shard_map(
        per_device, mesh=mesh, in_specs=in_specs, out_specs=out_specs, check_vma=False
    )
```

```python
import functools
import math

import jax
import jax.numpy as jnp
from jax import lax
from jax.experimental import pallas as pl
from jax.experimental.pallas import tpu as pltpu
from jax.sharding import PartitionSpec as P


LANES = 128
STEPS = 3
ROUTES = ("direct", "direct", "x", "y")

NT = (((1,), (1,)), ((), ()))
KERNEL_VMEM = pltpu.CompilerParams(vmem_limit_bytes=24_000_000)
ALL_VMEM = pltpu.CompilerParams(vmem_limit_bytes=66_000_000)
HBM = pl.BlockSpec(memory_space=pltpu.HBM)
VMEM = pl.BlockSpec(memory_space=pltpu.VMEM)
SMEM = pl.BlockSpec(memory_space=pltpu.SMEM)
ANY = pl.BlockSpec(memory_space=pl.ANY)


def swap_cores(x, count):
    return lax.ppermute(x, "tile", [(t, t ^ 1) for t in range(count)])


def identity(dtype):
    rows = lax.broadcasted_iota(jnp.int32, (LANES, LANES), 0)
    cols = lax.broadcasted_iota(jnp.int32, (LANES, LANES), 1)
    return (rows == cols).astype(jnp.float32).astype(dtype)


def turned(x):
    return lax.dot_general(identity(x.dtype), x, NT, preferred_element_type=jnp.float32)


def counts_kernel(scalars, counts_ref, mine_ref, other_ref, library_ref):
    genes = mine_ref.shape[1]
    total = None
    for side, target in ((scalars[0], mine_ref), (1 - scalars[0], other_ref)):
        part = counts_ref[0, :, pl.ds(pl.multiple_of(side * genes, genes), genes)]
        target[...] = part.astype(jnp.float32).astype(jnp.bfloat16)
        for g in range(0, genes, LANES):
            total = part[:, :LANES] if total is None else total + part[:, g : g + LANES]
    ones = jnp.ones((8, LANES), jnp.bfloat16)
    total = total.astype(jnp.float32).astype(jnp.bfloat16)
    library_ref[...] = lax.dot_general(ones, total, NT, preferred_element_type=jnp.float32)[:1]


def small_counts(scalars, counts):
    row_count, col_count, genes = counts.shape
    bins = row_count * col_count
    small = pl.BlockSpec((col_count, genes // 2), lambda r, s: (r, 0))
    return pl.pallas_call(
        counts_kernel,
        grid_spec=pltpu.PrefetchScalarGridSpec(
            num_scalar_prefetch=1,
            grid=(row_count,),
            in_specs=[pl.BlockSpec((1, col_count, genes), lambda r, s: (r, 0, 0))],
            out_specs=[small, small, pl.BlockSpec((1, col_count), lambda r, s: (0, r))],
        ),
        out_shape=[jax.ShapeDtypeStruct((bins, genes // 2), jnp.bfloat16)] * 2
        + [jax.ShapeDtypeStruct((1, bins), jnp.float32)],
        compiler_params=ALL_VMEM,
        name="small_counts",
        cost_estimate=pl.CostEstimate(flops=0, bytes_accessed=counts.size * 6, transcendentals=0),
    )(scalars, counts)


def weights_kernel(scalars, mine_ref, came_ref, *rest):
    parts, rows = rest[:-1], rest[-1]
    core = scalars[0]
    share, genes = mine_ref.shape[0], rows.shape[1]
    lanes = pl.ds(pl.multiple_of(core * genes, genes), genes)
    rows[pl.ds(pl.multiple_of(core * share, 16), share), :] = mine_ref[:, lanes]
    rows[pl.ds(pl.multiple_of((1 - core) * share, 16), share), :] = came_ref[:, lanes]
    for j, part in enumerate(parts):
        for b in range(rows.shape[0] // LANES):
            block = rows[b * LANES : (b + 1) * LANES, j * LANES : (j + 1) * LANES]
            part[b] = turned(block).astype(jnp.bfloat16)


def turn_weights(scalars, mine, came):
    share, genes = mine.shape
    blocks = genes // 2 // LANES
    part = jax.ShapeDtypeStruct((2 * share // LANES, LANES, LANES), jnp.bfloat16)
    return pl.pallas_call(
        weights_kernel,
        in_specs=[SMEM, VMEM, VMEM],
        out_specs=[VMEM] * blocks,
        out_shape=[part] * blocks,
        scratch_shapes=[pltpu.VMEM((2 * share, genes // 2), jnp.bfloat16)],
        compiler_params=ALL_VMEM,
        name="turn_weights",
        cost_estimate=pl.CostEstimate(flops=0, bytes_accessed=mine.size * 6, transcendentals=0),
    )(scalars, mine, came)


def block_copies(own_rows, cols, block, scalars, selection, features, halos, counts, fs, cs, f_sem, c_sem):
    core, parity = scalars[0], scalars[2]
    own_bins = own_rows * cols
    reads = selection.shape[1]
    row = core * (selection.shape[0] // 2) + block
    half_blocks = halos[0].shape[1] // LANES
    spans = ((0, cols), (cols, own_bins), (cols + own_bins, own_bins), (cols + 2 * own_bins, cols))

    def feature_copy(place, k, source, feature_block):
        at, size = spans[place]
        lanes = pl.ds(pl.multiple_of(feature_block * LANES, LANES), LANES)
        return pltpu.make_async_copy(
            source.at[:, lanes], fs.at[pl.ds(at, size), pl.ds(k * LANES, LANES)], f_sem.at[place, k]
        )

    def count_copy(side, source):
        return pltpu.make_async_copy(
            source.at[:, pl.ds(block * LANES, LANES)], cs.at[pl.ds(side * own_bins, own_bins)], c_sem.at[side]
        )

    for this in range(2):

        @pl.when(core == this)
        def _():
            near, far = features if this == 0 else features[::-1]
            top, bottom = (halos[:2], halos[2:]) if this == 0 else (halos[2:], halos[:2])
            for k in range(reads):
                chosen = selection[row, k]
                feature_copy(1, k, near, chosen).start()
                feature_copy(2, k, far, chosen).start()
                upper = jnp.where(chosen >= half_blocks, 1, 0)
                for held in range(2):

                    @pl.when((upper == parity) == (held == 0))
                    def _():
                        feature_copy(0, k, top[held], chosen - upper * half_blocks).start()
                        feature_copy(3, k, bottom[held], chosen - upper * half_blocks).start()

            for side, source in enumerate(counts if this == 0 else counts[::-1]):
                count_copy(side, source).start()

    def wait():
        for place in range(4):
            for k in range(reads):
                feature_copy(place, k, features[0] if 0 < place < 3 else halos[0], 0).wait()
        for side in range(2):
            count_copy(side, counts[0]).wait()

    return wait


def load_kernel(plan, scalars, selection, *rest):
    own_rows, cols, block, gene_total = plan
    features, halos, counts, libraries, rest = rest[:2], rest[2:6], rest[6:8], rest[8], rest[9:]
    fs, cs, ls, f_sem, c_sem = rest
    wait = block_copies(own_rows, cols, block, scalars, selection, features, halos, counts, fs, cs, f_sem, c_sem)
    own_bins = own_rows * cols
    core = scalars[0]
    total = libraries[0]
    for i in range(1, libraries.shape[0]):
        total += libraries[i]
    sizes = (total + 1.0) / gene_total
    ls[:, pl.ds(pl.multiple_of(core * own_bins, own_bins), own_bins)] = sizes[:1]
    ls[:, pl.ds(pl.multiple_of((1 - core) * own_bins, own_bins), own_bins)] = sizes[1:]
    wait()


def loaded(bins, cols, reads):
    return [
        pltpu.VMEM((bins + 2 * cols, reads * LANES), jnp.bfloat16),
        pltpu.VMEM((bins, LANES), jnp.bfloat16),
    ]


def load_block(scalars, selection, features, halos, counts, libraries, block, own_rows, cols, gene_total):
    bins, reads = 2 * own_rows * cols, selection.shape[1]
    return pl.pallas_call(
        functools.partial(load_kernel, (own_rows, cols, block, gene_total)),
        in_specs=[SMEM] * 2 + [HBM] * 8 + [VMEM],
        out_specs=[VMEM] * 3,
        out_shape=loaded(bins, cols, reads) + [pltpu.VMEM((1, bins), jnp.float32)],
        scratch_shapes=[pltpu.SemaphoreType.DMA((4, reads)), pltpu.SemaphoreType.DMA((2,))],
        compiler_params=KERNEL_VMEM,
        name="load_block",
        cost_estimate=pl.CostEstimate(flops=0, bytes_accessed=12 * 2**20, transcendentals=0),
    )(scalars, selection, *features, *halos, *counts, libraries)


def grad_kernel(plan, scalars, selection, fs, cs, ls, *rest):
    own_rows, cols, following, pieces, piece_blocks = plan
    features, halos, counts, rest = rest[:2], rest[2:6], rest[6:8], rest[8:]
    w_parts, g_parts, rest = rest[:pieces], rest[pieces : 2 * pieces], rest[2 * pieces :]
    wait_next = None
    if following is not None:
        next_fs, next_cs, rest = rest[0], rest[1], rest[2:]
    wv, wl, et, acc, gb, f_sem, c_sem, w_sem, out_sem = rest
    rows = 2 * own_rows
    reads = selection.shape[1]

    def first_block(p):
        return (scalars[1] ^ p) * piece_blocks if pieces > 1 else 0

    weight_copies = [
        pltpu.make_async_copy(w_parts[p], wv.at[pl.ds(first_block(p), piece_blocks)], w_sem.at[p])
        for p in range(pieces)
    ]
    for copy in weight_copies:
        copy.start()
    if following is not None:
        wait_next = block_copies(
            own_rows, cols, following, scalars, selection, features, halos, counts, next_fs, next_cs, f_sem, c_sem
        )
    for copy in weight_copies:
        copy.wait()
    for d in range(STEPS):
        for e in range(STEPS):
            for k in range(reads):
                wl[d, e * LANES : (e + 1) * LANES, k * LANES : (k + 1) * LANES] = wv[(STEPS * d + e) * reads + k]

    lane = lax.broadcasted_iota(jnp.int32, (LANES, cols), 1)

    def from_left(x):
        return jnp.where(lane > 0, pltpu.roll(x, 1, 1), 0.0)

    def from_right(x):
        return jnp.where(lane < cols - 1, pltpu.roll(x, cols - 1, 1), 0.0)

    def products(r):
        total = None
        for d in range(STEPS):
            one = lax.dot_general(
                wl[d], fs[pl.ds((r + d) * cols, cols), :], NT, preferred_element_type=jnp.float32
            )
            total = one if total is None else total + one
        return total

    def finish(r, sums):
        here = slice(r * cols, (r + 1) * cols)
        logits = from_left(sums[:LANES]) + sums[LANES : 2 * LANES] + from_right(sums[2 * LANES :])
        excess = ls[:, here] * jnp.exp(logits) - turned(cs[here, :])
        et[:LANES, here] = from_right(excess).astype(jnp.bfloat16)
        et[LANES : 2 * LANES, here] = excess.astype(jnp.bfloat16)
        et[2 * LANES :, here] = from_left(excess).astype(jnp.bfloat16)

    acc[0] = products(0)
    for r in range(1, rows):
        acc[r % 2] = products(r)
        finish(r - 1, acc[(r - 1) % 2])
    finish(rows - 1, acc[(rows - 1) % 2])

    def row_step(d, carry):
        span = pl.ds(pl.multiple_of(d * cols, cols), rows * cols)
        grad = jnp.dot(et[...], fs[span, :], preferred_element_type=jnp.float32)
        for e in range(STEPS):
            for k in range(reads):
                gb[(STEPS * d + e) * reads + k] = grad[
                    e * LANES : (e + 1) * LANES, k * LANES : (k + 1) * LANES
                ].astype(jnp.bfloat16)
        return carry

    lax.fori_loop(0, STEPS, row_step, 0)

    stores = [
        pltpu.make_async_copy(gb.at[pl.ds(first_block(p), piece_blocks)], g_parts[p], out_sem.at[p])
        for p in range(pieces)
    ]
    for copy in stores:
        copy.start()
    if wait_next is not None:
        wait_next()
    for copy in stores:
        copy.wait()


def block_gradient(scalars, selection, held, features, halos, counts, w_parts, following, own_rows, cols):
    pieces = len(w_parts)
    piece_blocks = w_parts[0].shape[0]
    reads = selection.shape[1]
    rows = 2 * own_rows
    taps = STEPS * STEPS * reads
    bins = rows * cols
    plan = (own_rows, cols, following, pieces, piece_blocks)
    more = [] if following is None else loaded(bins, cols, reads)
    part = pltpu.HBM((piece_blocks, LANES, LANES), jnp.bfloat16)
    return pl.pallas_call(
        functools.partial(grad_kernel, plan),
        in_specs=[SMEM] * 2 + [VMEM] * 3 + [HBM] * 8 + [ANY] * pieces,
        out_specs=[HBM] * pieces + [VMEM] * len(more),
        scratch_shapes=[
            pltpu.VMEM((taps, LANES, LANES), jnp.bfloat16),
            pltpu.VMEM((STEPS, STEPS * LANES, reads * LANES), jnp.bfloat16),
            pltpu.VMEM((STEPS * LANES, bins), jnp.bfloat16),
            pltpu.VMEM((2, STEPS * LANES, cols), jnp.float32),
            pltpu.VMEM((taps, LANES, LANES), jnp.bfloat16),
            pltpu.SemaphoreType.DMA((4, reads)),
            pltpu.SemaphoreType.DMA((2,)),
            pltpu.SemaphoreType.DMA((pieces,)),
            pltpu.SemaphoreType.DMA((pieces,)),
        ],
        out_shape=[part] * pieces + more,
        compiler_params=KERNEL_VMEM,
        name="block_gradient",
        cost_estimate=pl.CostEstimate(
            flops=4 * taps * LANES * LANES * bins, bytes_accessed=10 * 2**20, transcendentals=LANES * bins
        ),
    )(scalars, selection, *held, *features, *halos, *counts, *w_parts)


def sum_kernel(scale, scalars, *rest):
    parts, (mine_ref, other_ref, rows) = rest[:-3], rest[-3:]
    core = scalars[0]
    share = mine_ref.shape[0]
    for b in range(parts[0].shape[0]):
        total = parts[0][b].astype(jnp.float32)
        for part in parts[1:]:
            total += part[b].astype(jnp.float32)
        rows[b * LANES : (b + 1) * LANES, :] = total.T * scale
    mine_ref[...] = rows[pl.ds(pl.multiple_of(core * share, 8), share), :]
    other_ref[...] = rows[pl.ds(pl.multiple_of((1 - core) * share, 8), share), :]


def summed(scalars, parts, share, scale):
    shape = jax.ShapeDtypeStruct((share, LANES), jnp.float32)
    return pl.pallas_call(
        functools.partial(sum_kernel, scale),
        in_specs=[SMEM] + [VMEM] * len(parts),
        out_specs=[VMEM] * 2,
        out_shape=[shape, shape],
        scratch_shapes=[pltpu.VMEM((2 * share, LANES), jnp.float32)],
        compiler_params=ALL_VMEM,
        name="summed",
        cost_estimate=pl.CostEstimate(flops=0, bytes_accessed=8 * share * LANES, transcendentals=0),
    )(scalars, *parts)


def place_kernel(base, aliased, scalars, *rest):
    parts, out, sem = rest[aliased:-2], rest[-2], rest[-1]
    core = scalars[0]
    core_genes = out.shape[1] // 2
    copies = []
    for i, part in enumerate(parts):
        side = core if i % 2 == 0 else 1 - core
        lanes = pl.ds(pl.multiple_of(side * core_genes + (base + i // 2) * LANES, LANES), LANES)
        copies.append(pltpu.make_async_copy(part, out.at[:, lanes], sem.at[i]))
    for copy in copies:
        copy.start()
    for copy in copies:
        copy.wait()


def placed(scalars, parts, base, out, share, genes):
    held = [] if out is None else [out]
    return pl.pallas_call(
        functools.partial(place_kernel, base, len(held)),
        in_specs=[SMEM] + [HBM] * len(held) + [VMEM] * len(parts),
        out_specs=HBM,
        out_shape=jax.ShapeDtypeStruct((share, genes), jnp.float32),
        scratch_shapes=[pltpu.SemaphoreType.DMA((len(parts),))],
        input_output_aliases={1: 0} if held else {},
        compiler_params=ALL_VMEM,
        name="placed",
        cost_estimate=pl.CostEstimate(flops=0, bytes_accessed=8 * share * LANES * len(parts), transcendentals=0),
    )(scalars, *held, *parts)


def exchanged(x, piece, count):
    return lax.ppermute(x, "tile", [(t, t ^ (2 * piece)) for t in range(count)])


def per_device(features, counts, selection, weights):
    row_count, col_count, width = features.shape
    local_genes = counts.shape[2]
    tiles, gene_parts = lax.axis_size("tile"), lax.axis_size("gene")
    gene_total = local_genes * gene_parts
    norm_scale = 1.0 / math.sqrt(row_count * tiles * col_count)
    bins = row_count * col_count
    me, gene_part = lax.axis_index("tile"), lax.axis_index("gene")
    core, chip, parity = me & 1, me >> 1, gene_part & 1
    scalars = jnp.stack([core, chip, parity]).astype(jnp.int32)
    core_genes = local_genes // 2
    core_blocks = core_genes // LANES
    share = weights.shape[0]
    chips = tiles // 2
    planned = chips == 4 and (2 * share) % LANES == 0 and len(ROUTES) == core_blocks

    flat = features.reshape(bins, width)
    if planned:
        came = swap_cores(weights, tiles)
    edge = lax.dynamic_slice(
        features, (core * (row_count - 1), 0, parity * (width // 2)), (1, col_count, width // 2)
    ).reshape(col_count, width // 2)
    outward = [(t, t + 1) for t in range(1, tiles - 1, 2)] + [(t, t - 1) for t in range(2, tiles, 2)]
    beside = [(g, g ^ 1) for g in range(gene_parts)]
    halo = lax.ppermute(edge, "tile", outward)
    halo_z = lax.ppermute(halo, "gene", beside)
    other_rows = swap_cores(flat, tiles)
    own_counts, away_counts, own_library = small_counts(scalars, counts)
    other_library = swap_cores(own_library, tiles)
    other_counts = swap_cores(away_counts, tiles)

    gathered = []
    if planned:
        for b, part in enumerate(turn_weights(scalars, weights, came)):
            got = {p: exchanged(part, p, tiles) for p in (1, 2)}
            source, way = {"direct": (part, 3), "x": (got[1], 2), "y": (got[2], 1)}[ROUTES[b]]
            gathered.append([part, got[1], got[2], exchanged(source, way, tiles)])
    else:
        full = lax.all_gather(weights, "tile", axis=0, tiled=True)
        mine = lax.dynamic_slice_in_dim(full, core * core_genes, core_genes, 1)
        gathered = [[part] for part in mine.reshape(-1, LANES, core_blocks, LANES).transpose(2, 0, 3, 1)]

    library = jnp.concatenate([own_library, other_library], axis=0)
    if gene_parts <= 4:
        around = [
            lax.ppermute(library, "gene", [(g, (g + i) % gene_parts) for g in range(gene_parts)])
            for i in range(1, gene_parts)
        ]
        libraries = jnp.stack([library] + around)
    else:
        libraries = lax.psum(library, "gene")[None]
    halos = (halo, halo_z, swap_cores(halo, tiles), swap_cores(halo_z, tiles))

    sources = tuple(
        tuple(pltpu.with_memory_space_constraint(x, pltpu.HBM) for x in group)
        for group in ((flat, other_rows), halos, (own_counts, other_counts))
    )
    *held, factors = load_block(scalars, selection, *sources, libraries, 0, row_count, col_count, gene_total)
    gradients = []
    for b, w_parts in enumerate(gathered):
        following = b + 1 if b + 1 < core_blocks else None
        results = block_gradient(
            scalars, selection, (*held, factors), *sources, w_parts, following, row_count, col_count
        )
        gradients.append(results[: len(w_parts)])
        held = results[len(w_parts) :]
    if not planned:
        part = jnp.stack([part for part, in gradients])
        part = part.transpose(1, 3, 0, 2).reshape(-1, core_genes).astype(jnp.float32)
        nothing = jnp.zeros_like(part)
        low, high = jnp.where(core == 0, part, nothing), jnp.where(core == 0, nothing, part)
        total = lax.psum_scatter(jnp.concatenate([low, high], axis=1), "tile", scatter_dimension=0, tiled=True)
        return total * norm_scale

    arrived = []
    for own, *others in gradients:
        arrived.append([own] + [exchanged(others[p - 1], p, tiles) for p in (1, 2, 3)])
    parts = []
    for pieces in arrived:
        mine, other = summed(scalars, pieces, share, norm_scale)
        parts += [mine, swap_cores(other, tiles)]
    out = placed(scalars, parts[:-2], 0, None, share, local_genes)
    return placed(scalars, parts[-2:], core_blocks - 1, out, share, local_genes)


def solution(mesh):
    in_specs = (P("tile", None, None), P("tile", None, "gene"), P("gene", None), P("tile", "gene"))
    out_specs = P("tile", "gene")

    return jax.shard_map(per_device, mesh=mesh, in_specs=in_specs, out_specs=out_specs, check_vma=False)
```

```python
import functools
import math

import jax
import jax.numpy as jnp
from jax import lax
from jax.experimental import pallas as pl
from jax.experimental.pallas import tpu as pltpu
from jax.sharding import PartitionSpec as P


LANES = 128
STEPS = 3
GROUPS = ((0,), (1,), (2, 3))

NT = (((1,), (1,)), ((), ()))
KERNEL_VMEM = pltpu.CompilerParams(vmem_limit_bytes=24_000_000)
ALL_VMEM = pltpu.CompilerParams(vmem_limit_bytes=66_000_000)
HBM = pl.BlockSpec(memory_space=pltpu.HBM)
VMEM = pl.BlockSpec(memory_space=pltpu.VMEM)
SMEM = pl.BlockSpec(memory_space=pltpu.SMEM)
ANY = pl.BlockSpec(memory_space=pl.ANY)


def in_hbm(x):
    return pltpu.with_memory_space_constraint(x, pltpu.HBM)


def swap_cores(x, count):
    return lax.ppermute(x, "tile", [(t, t ^ 1) for t in range(count)])


def identity(dtype):
    rows = lax.broadcasted_iota(jnp.int32, (LANES, LANES), 0)
    cols = lax.broadcasted_iota(jnp.int32, (LANES, LANES), 1)
    return (rows == cols).astype(jnp.float32).astype(dtype)


def turned(x):
    return lax.dot_general(identity(x.dtype), x, NT, preferred_element_type=jnp.float32)


def counts_kernel(scalars, counts_ref, mine_ref, other_ref, library_ref):
    genes = mine_ref.shape[1]
    total = None
    for side, target in ((scalars[0], mine_ref), (1 - scalars[0], other_ref)):
        part = counts_ref[0, :, pl.ds(pl.multiple_of(side * genes, genes), genes)]
        target[...] = part.astype(jnp.float32).astype(jnp.bfloat16)
        for g in range(0, genes, LANES):
            total = part[:, :LANES] if total is None else total + part[:, g : g + LANES]
    ones = jnp.ones((8, LANES), jnp.bfloat16)
    total = total.astype(jnp.float32).astype(jnp.bfloat16)
    library_ref[...] = lax.dot_general(ones, total, NT, preferred_element_type=jnp.float32)[:1]


def small_counts(scalars, counts):
    row_count, col_count, genes = counts.shape
    bins = row_count * col_count
    small = pl.BlockSpec((col_count, genes // 2), lambda r, s: (r, 0))
    return pl.pallas_call(
        counts_kernel,
        grid_spec=pltpu.PrefetchScalarGridSpec(
            num_scalar_prefetch=1,
            grid=(row_count,),
            in_specs=[pl.BlockSpec((1, col_count, genes), lambda r, s: (r, 0, 0))],
            out_specs=[small, small, pl.BlockSpec((1, col_count), lambda r, s: (0, r))],
        ),
        out_shape=[jax.ShapeDtypeStruct((bins, genes // 2), jnp.bfloat16)] * 2
        + [jax.ShapeDtypeStruct((1, bins), jnp.float32)],
        compiler_params=ALL_VMEM,
        name="small_counts",
        cost_estimate=pl.CostEstimate(flops=0, bytes_accessed=counts.size * 6, transcendentals=0),
    )(scalars, counts)


def weights_kernel(scalars, mine_ref, came_ref, *rest):
    parts, rows = rest[:-1], rest[-1]
    core = scalars[0]
    share, genes = mine_ref.shape[0], rows.shape[1]
    lanes = pl.ds(pl.multiple_of(core * genes, genes), genes)
    rows[pl.ds(pl.multiple_of(core * share, 16), share), :] = mine_ref[:, lanes]
    rows[pl.ds(pl.multiple_of((1 - core) * share, 16), share), :] = came_ref[:, lanes]
    for part, group in zip(parts, GROUPS):
        for i, j in enumerate(group):
            for b in range(rows.shape[0] // LANES):
                block = rows[b * LANES : (b + 1) * LANES, j * LANES : (j + 1) * LANES]
                part[i, b] = turned(block).astype(jnp.bfloat16)


def turn_weights(scalars, mine, came):
    share, genes = mine.shape
    shape = (2 * share // LANES, LANES, LANES)
    return pl.pallas_call(
        weights_kernel,
        in_specs=[SMEM, VMEM, VMEM],
        out_specs=[VMEM] * len(GROUPS),
        out_shape=[jax.ShapeDtypeStruct((len(group),) + shape, jnp.bfloat16) for group in GROUPS],
        scratch_shapes=[pltpu.VMEM((2 * share, genes // 2), jnp.bfloat16)],
        compiler_params=ALL_VMEM,
        name="turn_weights",
        cost_estimate=pl.CostEstimate(flops=0, bytes_accessed=mine.size * 6, transcendentals=0),
    )(scalars, mine, came)


def block_copies(own_rows, cols, block, scalars, selection, features, halos, counts, fs, cs, f_sem, c_sem):
    core = scalars[0]
    own_bins = own_rows * cols
    reads = selection.shape[1]
    row = core * (selection.shape[0] // 2) + block
    spans = ((0, cols), (cols, own_bins), (cols + own_bins, own_bins), (cols + 2 * own_bins, cols))

    def feature_copy(place, k, source, feature_block):
        at, size = spans[place]
        lanes = pl.ds(pl.multiple_of(feature_block * LANES, LANES), LANES)
        return pltpu.make_async_copy(
            source.at[:, lanes], fs.at[pl.ds(at, size), pl.ds(k * LANES, LANES)], f_sem.at[place, k]
        )

    def count_copy(side, source):
        return pltpu.make_async_copy(
            source.at[:, pl.ds(block * LANES, LANES)], cs.at[pl.ds(side * own_bins, own_bins)], c_sem.at[side]
        )

    for this in range(2):

        @pl.when(core == this)
        def _():
            near, far = features if this == 0 else features[::-1]
            for k in range(reads):
                chosen = selection[row, k]
                feature_copy(1, k, near, chosen).start()
                feature_copy(2, k, far, chosen).start()
                feature_copy(0, k, halos[this], chosen).start()
                feature_copy(3, k, halos[1 - this], chosen).start()

            for side, source in enumerate(counts if this == 0 else counts[::-1]):
                count_copy(side, source).start()

    def wait():
        for place in range(4):
            for k in range(reads):
                feature_copy(place, k, features[0] if 0 < place < 3 else halos[0], 0).wait()
        for side in range(2):
            count_copy(side, counts[0]).wait()

    return wait


def load_kernel(plan, scalars, selection, *rest):
    own_rows, cols, block, gene_total = plan
    features, halos, counts, libraries, rest = rest[:2], rest[2:4], rest[4:6], rest[6:8], rest[8:]
    fs, cs, ls, f_sem, c_sem = rest
    wait = block_copies(own_rows, cols, block, scalars, selection, features, halos, counts, fs, cs, f_sem, c_sem)
    own_bins = own_rows * cols
    core = scalars[0]
    sizes = (libraries[0][...] + libraries[1][...] + 1.0) / gene_total
    ls[:, pl.ds(pl.multiple_of(core * own_bins, own_bins), own_bins)] = sizes[:1]
    ls[:, pl.ds(pl.multiple_of((1 - core) * own_bins, own_bins), own_bins)] = sizes[1:]
    wait()


def loaded(bins, cols, reads):
    return [
        pltpu.VMEM((bins + 2 * cols, reads * LANES), jnp.bfloat16),
        pltpu.VMEM((bins, LANES), jnp.bfloat16),
    ]


def load_block(scalars, selection, features, halos, counts, libraries, block, own_rows, cols, gene_total):
    bins, reads = 2 * own_rows * cols, selection.shape[1]
    return pl.pallas_call(
        functools.partial(load_kernel, (own_rows, cols, block, gene_total)),
        in_specs=[SMEM] * 2 + [HBM] * 6 + [VMEM] * 2,
        out_specs=[VMEM] * 3,
        out_shape=loaded(bins, cols, reads) + [pltpu.VMEM((1, bins), jnp.float32)],
        scratch_shapes=[pltpu.SemaphoreType.DMA((4, reads)), pltpu.SemaphoreType.DMA((2,))],
        compiler_params=KERNEL_VMEM,
        name="load_block",
        cost_estimate=pl.CostEstimate(flops=0, bytes_accessed=12 * 2**20, transcendentals=0),
    )(scalars, selection, *features, *halos, *counts, *libraries)


def grad_kernel(plan, scalars, selection, fs, cs, ls, *rest):
    own_rows, cols, offset, following, pieces, piece_blocks = plan
    features, halos, counts, rest = rest[:2], rest[2:4], rest[4:6], rest[6:]
    w_parts, g_parts, rest = rest[:pieces], rest[pieces : 2 * pieces], rest[2 * pieces :]
    wait_next = None
    if following is not None:
        next_fs, next_cs, rest = rest[0], rest[1], rest[2:]
    wv, wl, et, acc, gb, f_sem, c_sem, w_sem, out_sem = rest
    rows = 2 * own_rows
    reads = selection.shape[1]

    def first_block(p):
        return (scalars[1] ^ p) * piece_blocks if pieces > 1 else 0

    weight_copies = [
        pltpu.make_async_copy(w_parts[p].at[offset], wv.at[pl.ds(first_block(p), piece_blocks)], w_sem.at[p])
        for p in range(pieces)
    ]
    for copy in weight_copies:
        copy.start()
    for copy in weight_copies:
        copy.wait()
    for d in range(STEPS):
        for e in range(STEPS):
            for k in range(reads):
                wl[d, e * LANES : (e + 1) * LANES, k * LANES : (k + 1) * LANES] = wv[(STEPS * d + e) * reads + k]

    if following is not None:
        wait_next = block_copies(
            own_rows, cols, following, scalars, selection, features, halos, counts, next_fs, next_cs, f_sem, c_sem
        )

    lane = lax.broadcasted_iota(jnp.int32, (LANES, cols), 1)

    def from_left(x):
        return jnp.where(lane > 0, pltpu.roll(x, 1, 1), 0.0)

    def from_right(x):
        return jnp.where(lane < cols - 1, pltpu.roll(x, cols - 1, 1), 0.0)

    def products(r):
        total = None
        for d in range(STEPS):
            one = lax.dot_general(
                wl[d], fs[pl.ds((r + d) * cols, cols), :], NT, preferred_element_type=jnp.float32
            )
            total = one if total is None else total + one
        return total

    def finish(r, sums):
        here = slice(r * cols, (r + 1) * cols)
        logits = from_left(sums[:LANES]) + sums[LANES : 2 * LANES] + from_right(sums[2 * LANES :])
        excess = ls[:, here] * jnp.exp(logits) - turned(cs[here, :])
        et[:LANES, here] = from_right(excess).astype(jnp.bfloat16)
        et[LANES : 2 * LANES, here] = excess.astype(jnp.bfloat16)
        et[2 * LANES :, here] = from_left(excess).astype(jnp.bfloat16)

    acc[0] = products(0)
    for r in range(1, rows):
        acc[r % 2] = products(r)
        finish(r - 1, acc[(r - 1) % 2])
    finish(rows - 1, acc[(rows - 1) % 2])

    def row_step(d, carry):
        span = pl.ds(pl.multiple_of(d * cols, cols), rows * cols)
        grad = jnp.dot(et[...], fs[span, :], preferred_element_type=jnp.float32)
        for e in range(STEPS):
            for k in range(reads):
                gb[(STEPS * d + e) * reads + k] = grad[
                    e * LANES : (e + 1) * LANES, k * LANES : (k + 1) * LANES
                ].astype(jnp.bfloat16)
        return carry

    lax.fori_loop(0, STEPS, row_step, 0)

    stores = [
        pltpu.make_async_copy(gb.at[pl.ds(first_block(p), piece_blocks)], g_parts[p], out_sem.at[p])
        for p in range(pieces)
    ]
    for copy in stores:
        copy.start()
    if wait_next is not None:
        wait_next()
    for copy in stores:
        copy.wait()


def block_gradient(scalars, selection, held, features, halos, counts, w_parts, offset, following, own_rows, cols):
    pieces = len(w_parts)
    piece_blocks = w_parts[0].shape[1]
    reads = selection.shape[1]
    rows = 2 * own_rows
    taps = STEPS * STEPS * reads
    bins = rows * cols
    plan = (own_rows, cols, offset, following, pieces, piece_blocks)
    more = [] if following is None else loaded(bins, cols, reads)
    part = pltpu.HBM((piece_blocks, LANES, LANES), jnp.bfloat16)
    return pl.pallas_call(
        functools.partial(grad_kernel, plan),
        in_specs=[SMEM] * 2 + [VMEM] * 3 + [HBM] * 6 + [ANY] * pieces,
        out_specs=[HBM] * pieces + [VMEM] * len(more),
        scratch_shapes=[
            pltpu.VMEM((taps, LANES, LANES), jnp.bfloat16),
            pltpu.VMEM((STEPS, STEPS * LANES, reads * LANES), jnp.bfloat16),
            pltpu.VMEM((STEPS * LANES, bins), jnp.bfloat16),
            pltpu.VMEM((2, STEPS * LANES, cols), jnp.float32),
            pltpu.VMEM((taps, LANES, LANES), jnp.bfloat16),
            pltpu.SemaphoreType.DMA((4, reads)),
            pltpu.SemaphoreType.DMA((2,)),
            pltpu.SemaphoreType.DMA((pieces,)),
            pltpu.SemaphoreType.DMA((pieces,)),
        ],
        out_shape=[part] * pieces + more,
        compiler_params=KERNEL_VMEM,
        name="block_gradient",
        cost_estimate=pl.CostEstimate(
            flops=4 * taps * LANES * LANES * bins, bytes_accessed=10 * 2**20, transcendentals=LANES * bins
        ),
    )(scalars, selection, *held, *features, *halos, *counts, *w_parts)


def sum_kernel(scale, blocks, scalars, *rest):
    parts, (mine_ref, other_ref, rows) = rest[:-3], rest[-3:]
    core = scalars[0]
    share = mine_ref.shape[0]
    pieces = len(parts) // blocks
    for j in range(blocks):
        for b in range(parts[0].shape[0]):
            total = parts[j * pieces][b].astype(jnp.float32)
            for part in parts[j * pieces + 1 : (j + 1) * pieces]:
                total += part[b].astype(jnp.float32)
            rows[b * LANES : (b + 1) * LANES, j * LANES : (j + 1) * LANES] = total.T * scale
    mine_ref[...] = rows[pl.ds(pl.multiple_of(core * share, 8), share), :]
    other_ref[...] = rows[pl.ds(pl.multiple_of((1 - core) * share, 8), share), :]


def summed(scalars, arrived, share, scale):
    blocks = len(arrived)
    parts = [part for pieces in arrived for part in pieces]
    shape = jax.ShapeDtypeStruct((share, blocks * LANES), jnp.float32)
    return pl.pallas_call(
        functools.partial(sum_kernel, scale, blocks),
        in_specs=[SMEM] + [VMEM] * len(parts),
        out_specs=[VMEM] * 2,
        out_shape=[shape, shape],
        scratch_shapes=[pltpu.VMEM((2 * share, blocks * LANES), jnp.float32)],
        compiler_params=ALL_VMEM,
        name="summed",
        cost_estimate=pl.CostEstimate(flops=0, bytes_accessed=8 * share * blocks * LANES, transcendentals=0),
    )(scalars, *parts)


def place_kernel(base, aliased, scalars, *rest):
    parts, out, sem = rest[aliased:-2], rest[-2], rest[-1]
    core = scalars[0]
    core_genes = out.shape[1] // 2
    copies = []
    for i, part in enumerate(parts):
        side = core if i % 2 == 0 else 1 - core
        lanes = pl.ds(pl.multiple_of(side * core_genes + base * LANES, LANES), part.shape[1])
        copies.append(pltpu.make_async_copy(part, out.at[:, lanes], sem.at[i]))
    for copy in copies:
        copy.start()
    for copy in copies:
        copy.wait()


def placed(scalars, parts, base, out, share, genes):
    held = [] if out is None else [out]
    return pl.pallas_call(
        functools.partial(place_kernel, base, len(held)),
        in_specs=[SMEM] + [HBM] * len(held) + [VMEM] * len(parts),
        out_specs=HBM,
        out_shape=jax.ShapeDtypeStruct((share, genes), jnp.float32),
        scratch_shapes=[pltpu.SemaphoreType.DMA((len(parts),))],
        input_output_aliases={1: 0} if held else {},
        compiler_params=ALL_VMEM,
        name="placed",
        cost_estimate=pl.CostEstimate(flops=0, bytes_accessed=8 * share * LANES * len(parts), transcendentals=0),
    )(scalars, *held, *parts)


def exchanged(x, piece, count):
    return lax.ppermute(x, "tile", [(t, t ^ (2 * piece)) for t in range(count)])


def per_device(features, counts, selection, weights):
    row_count, col_count, width = features.shape
    local_genes = counts.shape[2]
    tiles, gene_parts = lax.axis_size("tile"), lax.axis_size("gene")
    gene_total = local_genes * gene_parts
    norm_scale = 1.0 / math.sqrt(row_count * tiles * col_count)
    bins = row_count * col_count
    me = lax.axis_index("tile")
    core, chip = me & 1, me >> 1
    scalars = jnp.stack([core, chip]).astype(jnp.int32)
    core_genes = local_genes // 2
    core_blocks = core_genes // LANES
    share = weights.shape[0]
    chips = tiles // 2
    planned = chips == 4 and (2 * share) % LANES == 0 and sum(map(len, GROUPS)) == core_blocks

    flat = features.reshape(bins, width)
    if planned:
        came = swap_cores(weights, tiles)
    edge = lax.dynamic_slice_in_dim(flat, core * (bins - col_count), col_count, 0)
    outward = [(t, t + 1) for t in range(1, tiles - 1, 2)] + [(t, t - 1) for t in range(2, tiles, 2)]
    halo = lax.ppermute(edge, "tile", outward)
    other_rows = swap_cores(flat, tiles)
    own_counts, away_counts, own_library = small_counts(scalars, counts)
    other_library = swap_cores(own_library, tiles)
    other_counts = swap_cores(away_counts, tiles)

    gathered = []
    if planned:
        for part in turn_weights(scalars, weights, came):
            got = {p: exchanged(part, p, tiles) for p in (3, 1, 2)}
            parts = [part] + [got[p] for p in (1, 2, 3)]
            gathered += [(parts, j) for j in range(part.shape[0])]
    else:
        full = lax.all_gather(weights, "tile", axis=0, tiled=True)
        mine = lax.dynamic_slice_in_dim(full, core * core_genes, core_genes, 1)
        full = mine.reshape(-1, LANES, core_blocks, LANES).transpose(2, 0, 3, 1)
        gathered = [([full], j) for j in range(core_blocks)]

    library = jnp.concatenate([own_library, other_library], axis=0)
    bits = gene_parts.bit_length() - 1
    if gene_parts == 1 << bits and bits > 0:
        for bit in range(bits):
            came = lax.ppermute(library, "gene", [(g, g ^ (1 << bit)) for g in range(gene_parts)])
            libraries = (library, came)
            library = library + came if bit + 1 < bits else library
    else:
        libraries = (lax.psum(library, "gene"), jnp.zeros_like(library))
    halos = (halo, swap_cores(halo, tiles))

    sources = tuple(
        tuple(in_hbm(x) for x in group)
        for group in ((flat, other_rows), halos, (own_counts, other_counts))
    )
    *held, factors = load_block(scalars, selection, *sources, libraries, 0, row_count, col_count, gene_total)
    gradients = []
    for b, (w_parts, offset) in enumerate(gathered):
        following = b + 1 if b + 1 < core_blocks else None
        results = block_gradient(
            scalars, selection, (*held, factors), *sources, w_parts, offset, following, row_count, col_count
        )
        gradients.append(results[: len(w_parts)])
        held = results[len(w_parts) :]
    if not planned:
        part = jnp.stack([part for part, in gradients])
        part = part.transpose(1, 3, 0, 2).reshape(-1, core_genes).astype(jnp.float32)
        nothing = jnp.zeros_like(part)
        low, high = jnp.where(core == 0, part, nothing), jnp.where(core == 0, nothing, part)
        total = lax.psum_scatter(jnp.concatenate([low, high], axis=1), "tile", scatter_dimension=0, tiled=True)
        return total * norm_scale

    arrived = []
    for own, *others in gradients:
        arrived.append([own] + [exchanged(others[p - 1], p, tiles) for p in (1, 2, 3)])
    out = None
    for group in (range(core_blocks - 1), range(core_blocks - 1, core_blocks)):
        mine, other = summed(scalars, [arrived[b] for b in group], share, norm_scale)
        parts = (mine, swap_cores(other, tiles))
        out = placed(scalars, parts, group[0], out, share, local_genes)
    return out


def solution(mesh):
    in_specs = (P("tile", None, None), P("tile", None, "gene"), P("gene", None), P("tile", "gene"))
    out_specs = P("tile", "gene")

    return jax.shard_map(per_device, mesh=mesh, in_specs=in_specs, out_specs=out_specs, check_vma=False)
```
